32 devices in a mesh: ax: 4 (over x, core), xs: 8 (over z, y).
Axes of the slice: x: 2, y: 2, z: 4, core: 2. Of those that a mesh axis runs over, the one named last changes fastest.
Arguments:
- concentrations_before: float32 [9, 48, 32, 1024], P(None, 'ax', 'xs'), may hold values from 0.05 to 1
- thermal_field_before: float32 [48, 32, 1024], P('ax', 'xs'), may hold values from 0.8 to 2.5
- flow_speed_vector: float32 [3, 48, 32, 1024], P(None, 'ax', 'xs'), may hold values from -4 to 4
- gap_indicator: int32 [48, 32, 1024], P('ax', 'xs'), may hold values 0 or 1
- destination_slice: int32 [48], replicated, may hold values from 0 to 47, as said below
- reaction_rate_constant: float32 [9], replicated, may hold values from 0.5 to 4
- threshold_kelvin: float32 [9], replicated, may hold values from 0.5 to 3
- reaction_coefficient_matrix: float32 [9, 9], replicated, may hold values from -2 to 2
- energy_release: float32 [9], replicated, may hold values from -4 to 4
- viewer_picture: float32 [32, 1024], P('xs', 'ax'), may hold values from 0 to 1.5
Outputs:
- concentrations_after: float32 [9, 48, 32, 1024], P(None, 'ax', 'xs')
- thermal_field_after: float32 [48, 32, 1024], P('ax', 'xs')
- image_error: float32 [32, 1024], P('xs', 'ax')
The draws below stay inside these ranges and needn't reach their ends.
Inputs may be any that keep to these rules, and one draw needn't show every extreme that they name: destination_slice[p] = p minus the number of 2 distinct merge positions (each in 1 to 47) at or before p, one of which lies in 1 to 12; so destination_slice is nondecreasing, lies in [p - 2, p], and each new plane from 0 to 45 receives between one and 3 old planes (more than two only where merge positions are adjacent).
All inputs are finite; a program needn't handle non-finite values. No bound on the sum of `gap_indicator` on one device may be relied on, other than what follows from the above.
Results may differ from the reference program's by a relative error of at most 0.000053.
Values sent between devices are 32-bit elements; how exact they have to be, the bound alone decides.
No kernel may reach another device: no remote copies, remote signals or barrier semaphores. Data moves between devices by JAX's collectives and lax.ppermute only.
A program may use at most 64 MiB of HBM per device.

```python
import math
import jax
import jax.numpy as jnp
from jax import lax

SPECIES_TOTAL = 9
CA = 12
MESH_ROWS_OUTER = 1024
LENGTHWISE_SLICES = 48
MESH_ROWS_INNER = 32


def draw_destination_slice(key, part):
    first_key = jax.random.fold_in(key, 11)
    order_key = jax.random.fold_in(key, 23)
    early = jax.random.randint(first_key, (), 1, CA + 1).astype(jnp.int32)
    order = (jax.random.permutation(order_key, LENGTHWISE_SLICES - 1) + 1).astype(jnp.int32)
    second = jnp.where(order[0] == early, order[1], order[0]).astype(jnp.int32)
    picks = jnp.stack([early, second])
    planes = jnp.arange(LENGTHWISE_SLICES, dtype=jnp.int32)
    merged = jnp.sum((picks[:, None] <= planes[None, :]).astype(jnp.int32), axis=0)
    return (planes - merged).astype(jnp.int32)


def plant(result, stream_key, smallest, high):
    extent = result.shape
    index_at = [jax.random.randint(jax.random.fold_in(stream_key, axis), (), 0, extent[axis]) for axis in range(len(extent))]
    result = result.at[tuple(index_at)].set(smallest)
    longest = extent.index(max(extent))
    index_at[longest] = (index_at[longest] + 1) % extent[longest]
    return result.at[tuple(index_at)].set(high)


def steps_of(own_key, dims, shards, low, high):
    gain = 1.0
    for position, blocks in shards:
        heights = jax.random.uniform(jax.random.fold_in(jax.random.fold_in(own_key, 6), position), (blocks,), jnp.float32, low / len(shards), high / len(shards))
        gain = gain * jnp.repeat(jnp.exp(heights), dims[position] // blocks).reshape((-1,) + (1,) * (len(dims) - 1 - position))
    return gain


def normal_values(stream_key, shape, deviation, reach, shards=(), held_as=jnp.bfloat16):
    values = deviation * jax.random.normal(stream_key, shape, jnp.float32)
    if shards:
        values = values * steps_of(stream_key, shape, shards, -0.22, 0.18)
    return jnp.clip(values, -reach, reach).astype(held_as)


def setup_inputs(seed: int = 0) -> dict:
    seeds = jax.random.split(jax.random.key(seed), 11)
    concentrations_before = jnp.clip(0.05 + 0.95 * jax.random.uniform(seeds[0], (SPECIES_TOTAL, LENGTHWISE_SLICES, MESH_ROWS_INNER, MESH_ROWS_OUTER), jnp.float32) ** steps_of(seeds[0], (SPECIES_TOTAL, LENGTHWISE_SLICES, MESH_ROWS_INNER, MESH_ROWS_OUTER), ((1, 4), (2, 8)), -0.2, 0.2), 0.05, 1.0)
    thermal_field_before = jnp.clip(0.8 + 1.7 * jax.random.uniform(seeds[1], (LENGTHWISE_SLICES, MESH_ROWS_INNER, MESH_ROWS_OUTER), jnp.float32) ** steps_of(seeds[1], (LENGTHWISE_SLICES, MESH_ROWS_INNER, MESH_ROWS_OUTER), ((0, 4), (1, 8)), -0.2, 0.2), 0.8, 2.5)
    flow_speed_vector = normal_values(seeds[2], (3, LENGTHWISE_SLICES, MESH_ROWS_INNER, MESH_ROWS_OUTER), 1.0, 4.0, ((1, 4), (2, 8)), jnp.float32)
    gap_indicator = plant((jax.random.randint(seeds[3], (LENGTHWISE_SLICES, MESH_ROWS_INNER, MESH_ROWS_OUTER), 0, 4) < 1).astype(jnp.int32), jax.random.fold_in(seeds[3], 1), 0, 1)
    destination_slice = draw_destination_slice(jax.random.fold_in(seeds[10], 71), 0)
    reaction_rate_constant = jnp.clip(jnp.exp(jax.random.uniform(seeds[5], (SPECIES_TOTAL,), jnp.float32, math.log(0.5), math.log(4.0))), 0.5, 4.0)
    threshold_kelvin = jnp.clip(jnp.exp(jax.random.uniform(seeds[6], (SPECIES_TOTAL,), jnp.float32, math.log(0.5), math.log(3.0))), 0.5, 3.0)
    reaction_coefficient_matrix = normal_values(seeds[7], (SPECIES_TOTAL, SPECIES_TOTAL), SPECIES_TOTAL ** -0.5, 2.0, (), jnp.float32)
    energy_release = normal_values(seeds[8], (SPECIES_TOTAL,), 1.0, 4.0, (), jnp.float32)
    viewer_picture = jnp.clip(1.5 * jax.random.uniform(seeds[9], (MESH_ROWS_INNER, MESH_ROWS_OUTER), jnp.float32) ** steps_of(seeds[9], (MESH_ROWS_INNER, MESH_ROWS_OUTER), ((0, 8), (1, 4)), -0.2, 0.2), 0.0, 1.5)
    return {"concentrations_before": concentrations_before, "thermal_field_before": thermal_field_before, "flow_speed_vector": flow_speed_vector, "gap_indicator": gap_indicator, "destination_slice": destination_slice, "reaction_rate_constant": reaction_rate_constant, "threshold_kelvin": threshold_kelvin, "reaction_coefficient_matrix": reaction_coefficient_matrix, "energy_release": energy_release, "viewer_picture": viewer_picture}


def remap_planes(extended, owner_part, first, count_new, fallback):
    targets = first + jnp.arange(count_new, dtype=jnp.int32)
    onehot = (owner_part[None, :] == targets[:, None]).astype(jnp.float32)
    summed = jnp.einsum("qp,cpyz->cqyz", onehot, extended, precision=lax.Precision.HIGHEST)
    counts = jnp.sum(onehot, axis=1)
    scaled = summed / jnp.maximum(counts, 1.0)[None, :, None, None]
    return jnp.where((counts > 0.0)[None, :, None, None], scaled, fallback)


def chemistry(center, reaction_rate_constant, threshold_kelvin, reaction_coefficient_matrix, energy_release):
    ys = center[:SPECIES_TOTAL]
    temp = center[SPECIES_TOTAL]
    rates = reaction_rate_constant[:, None, None, None] * jnp.exp(-threshold_kelvin[:, None, None, None] / temp[None]) * ys * jnp.roll(ys, -1, axis=0)
    source = jnp.einsum("sr,ryz->syz", reaction_coefficient_matrix, rates.reshape(SPECIES_TOTAL, rates.shape[1], -1), precision=lax.Precision.HIGHEST).reshape(rates.shape)
    warming_source = jnp.einsum("r,ryz->yz", energy_release, rates.reshape(SPECIES_TOTAL, rates.shape[1], -1), precision=lax.Precision.HIGHEST).reshape(rates.shape[1:])
    return source, warming_source


def reference(concentrations_before, thermal_field_before, flow_speed_vector, gap_indicator, destination_slice, reaction_rate_constant, threshold_kelvin, reaction_coefficient_matrix, energy_release, viewer_picture):
    earlier_fields = jnp.concatenate([concentrations_before, thermal_field_before[None]], axis=0)
    remapped = remap_planes(earlier_fields, destination_slice, jnp.int32(0), LENGTHWISE_SLICES, earlier_fields)
    padded = jnp.pad(remapped, ((0, 0), (1, 1), (1, 1), (1, 1)))
    upper_a = padded[:, 2:, 1:-1, 1:-1]
    lower_a = padded[:, :-2, 1:-1, 1:-1]
    upper_y = padded[:, 1:-1, 2:, 1:-1]
    lower_y = padded[:, 1:-1, :-2, 1:-1]
    upper_z = padded[:, 1:-1, 1:-1, 2:]
    lower_z = padded[:, 1:-1, 1:-1, :-2]
    lap = upper_a + lower_a + upper_y + lower_y + upper_z + lower_z - 6.0 * remapped
    adv = 0.5 * (flow_speed_vector[0][None] * (upper_a - lower_a) + flow_speed_vector[1][None] * (upper_y - lower_y) + flow_speed_vector[2][None] * (upper_z - lower_z))
    advective_current = remapped + 0.1 * lap - 0.2 * adv
    source, warming_source = chemistry(remapped, reaction_rate_constant, threshold_kelvin, reaction_coefficient_matrix, energy_release)
    fluid_blend = (1 - gap_indicator).astype(jnp.float32)
    concentrations_after = advective_current[:SPECIES_TOTAL] + 0.5 * fluid_blend[None] * source
    thermal_field_after = advective_current[SPECIES_TOTAL] + 0.5 * fluid_blend * warming_source
    glow_picture = jnp.sum(fluid_blend * concentrations_after[4] * thermal_field_after, axis=0) / LENGTHWISE_SLICES
    return concentrations_after, thermal_field_after, glow_picture - viewer_picture
```

```python
import functools

import jax
import jax.numpy as jnp
from jax import lax
from jax.experimental import pallas as pl
from jax.experimental.pallas import tpu as pltpu
from jax.sharding import PartitionSpec as P

SPECIES = 9
FIELDS = SPECIES + 1
GLOW = 4
SHIFT = 2
LANES = 128
VMEM = pl.BlockSpec(memory_space=pltpu.VMEM)
SMEM = pl.BlockSpec(memory_space=pltpu.SMEM)
GRANT = 16 << 20
ANY = pl.BlockSpec(memory_space=pl.ANY)


def tiled(x):
    *lead, rows, columns = x.shape
    n = len(lead)
    split = x.reshape(*lead, rows, columns // LANES, LANES)
    order = tuple(range(n)) + (n + 1, n, n + 2)
    return split.transpose(order).reshape(*lead, rows * columns // LANES, LANES)


def untiled(x, rows):
    *lead, height, _ = x.shape
    n = len(lead)
    split = x.reshape(*lead, height // rows, rows, LANES)
    order = tuple(range(n)) + (n + 1, n, n + 2)
    return split.transpose(order).reshape(*lead, rows, height // rows * LANES)


def swaps(count, offset):
    pairs = []
    for i in range(offset, count - 1, 2):
        pairs += [(i, i + 1), (i + 1, i)]
    return pairs


def remap_weights(owner, plane):
    total = owner.shape[0]
    inside = jnp.logical_and(plane >= 0, plane < total)
    hits = []
    for k in range(SHIFT + 1):
        p = plane + k
        mine = owner[jnp.clip(p, 0, total - 1)] == plane
        hits.append(jnp.where(inside & (p < total) & mine, 1.0, 0.0))
    count = hits[0] + hits[1] + hits[2]
    share = jnp.where(count > 2.5, 1.0 / 3.0, jnp.where(count > 1.5, 0.5, 1.0))
    kept = jnp.where(jnp.logical_and(inside, count < 0.5), 1.0, 0.0)
    return hits[0] * share + kept, hits[1] * share, hits[2] * share


def mix(weights, values):
    return weights[0] * values[0] + weights[1] * values[1] + weights[2] * values[2]


def old_field(c, t, f):
    return t if f == SPECIES else c.at[f]


def edge_starts(rows):
    even = lax.rem(lax.axis_index("xs"), 2) == 0
    return jnp.where(even, rows - 1, 0), jnp.where(even, 0, rows - 1)


def send_kernel(rows, owner, c, t, to_even, to_odd, up_even, up_odd):
    planes, height, _ = t.shape
    tiles = height // rows
    first = lax.axis_index("ax") * planes
    starts = edge_starts(rows)
    shares = [remap_weights(owner, first + j) for j in range(planes - SHIFT)]
    for f in range(FIELDS):
        ref = old_field(c, t, f)
        for start, out in zip(starts, (to_even, to_odd)):
            edge = [ref[p, pl.ds(start, tiles, stride=rows), :] for p in range(planes)]
            for j in range(planes - SHIFT):
                out[f, j] = mix(shares[j], edge[j : j + 3])
    even = lax.rem(lax.axis_index("ax"), 2) == 0
    depth = SHIFT + 1
    for f in range(FIELDS):
        ref = old_field(c, t, f)
        up_even[f] = ref[pl.ds(jnp.where(even, planes - depth, 0), depth)]
        up_odd[f] = ref[pl.ds(jnp.where(even, 0, planes - depth), depth)]


def late_kernel(rows, owner, c, t, got_even, got_odd, to_even, to_odd):
    planes, height, _ = t.shape
    tiles = height // rows
    first = lax.axis_index("ax") * planes
    starts = edge_starts(rows)
    even = lax.rem(lax.axis_index("ax"), 2) == 0
    shares = [remap_weights(owner, first + planes - SHIFT + j) for j in range(SHIFT)]
    for f in range(FIELDS):
        ref = old_field(c, t, f)
        for start, out in zip(starts, (to_even, to_odd)):
            where = pl.ds(start, tiles, stride=rows)
            edge = [ref[planes - SHIFT + p, where, :] for p in range(SHIFT)]
            for p in range(SHIFT):
                edge.append(jnp.where(even, got_even[f, p, where, :], got_odd[f, p, where, :]))
            for j in range(SHIFT):
                out[f, j] = mix(shares[j], edge[j : j + 3])


def main_kernel(
    rows, owner, rate, threshold, matrix, release, c, t, got_even, got_odd, flow, gap, out, held
):
    planes, height, _ = t.shape
    blocks = height // 8
    first = lax.axis_index("ax") * planes
    even = lax.rem(lax.axis_index("ax"), 2) == 0
    body = pl.ds(8, height)
    zeros = jnp.zeros((8, LANES), jnp.float32)

    def clear(j, carry):
        for f in range(FIELDS):
            held[f, j, 0:8] = zeros
            held[f, j, 8 + height : 16 + height] = zeros
        return carry

    lax.fori_loop(1, planes + 1, clear, 0)

    def inner(j, carry):
        share = remap_weights(owner, first + j)
        for f in range(FIELDS):
            ref = old_field(c, t, f)
            held[f, j + 1, body] = mix(share, [ref[j + k] for k in range(3)])
        return carry

    lax.fori_loop(0, planes - SHIFT, inner, 0)
    low = remap_weights(owner, first - 1)
    high = [remap_weights(owner, first + planes - SHIFT + j) for j in range(SHIFT + 1)]
    for f in range(FIELDS):
        ref = old_field(c, t, f)
        lower = jnp.where(even, got_odd[f, SHIFT], got_even[f, SHIFT])
        held[f, 0, body] = mix(low, [lower, ref[0], ref[1]])
        chain = [ref[planes - SHIFT + p] for p in range(SHIFT)]
        for p in range(SHIFT + 1):
            chain.append(jnp.where(even, got_even[f, p], got_odd[f, p]))
        for j in range(SHIFT + 1):
            held[f, planes - SHIFT + 1 + j, body] = mix(high[j], chain[j : j + 3])

    lane = lax.broadcasted_iota(jnp.int32, (8, LANES), 1)
    row = lax.rem(lax.broadcasted_iota(jnp.int32, (8, LANES), 0), rows)
    first_lane, last_lane = lane == 0, lane == LANES - 1
    first_row, last_row = row == 0, row == rows - 1

    def plane_step(p, carry):
        for b in range(blocks):
            here = pl.ds(8 * b, 8)
            va, vy, vz = (0.1 * flow[d, p, here] for d in range(3))
            up_y = jnp.where(last_row, 0.0, 0.1 - vy)
            low_y = jnp.where(first_row, 0.0, 0.1 + vy)
            up_a, low_a, up_z, low_z = 0.1 - va, 0.1 + va, 0.1 - vz, 0.1 + vz

            def at(f, plane, offset):
                return held[f, plane, pl.ds(8 + 8 * b + offset, 8)]

            flux, mid = [], []
            for f in range(FIELDS):
                m = at(f, p + 1, 0)
                above_z = jnp.where(first_lane, at(f, p + 1, rows), m)
                below_z = jnp.where(last_lane, at(f, p + 1, -rows), m)
                flux.append(
                    0.4 * m
                    + up_a * at(f, p + 2, 0)
                    + low_a * at(f, p, 0)
                    + up_y * at(f, p + 1, 1)
                    + low_y * at(f, p + 1, -1)
                    + up_z * pltpu.roll(above_z, LANES - 1, 1)
                    + low_z * pltpu.roll(below_z, 1, 1)
                )
                mid.append(m)
            inverse = 1.0 / mid[SPECIES]
            rates = []
            for r in range(SPECIES):
                speed = rate[r] * jnp.exp(-threshold[r] * inverse)
                rates.append(speed * mid[r] * mid[(r + 1) % SPECIES])
            half_gas = 0.5 * (1 - gap[p, here]).astype(jnp.float32)
            for f in range(FIELDS):
                parts = [
                    (release[r] if f == SPECIES else matrix[f, r]) * rates[r]
                    for r in range(SPECIES)
                ]
                out[f, p, here] = flux[f] + half_gas * sum(parts[1:], parts[0])
        return carry

    lax.fori_loop(0, planes, plane_step, 0)


def finished(rows, f, p, partial, flow, halos):
    e_main, o_main, e_late, o_late = halos
    planes, height = partial.shape[1:3]
    tiles = height // rows
    even = lax.rem(lax.axis_index("xs"), 2) == 0
    late = p >= planes - SHIFT
    e = e_late[f, p - planes + SHIFT] if late else e_main[f, p]
    o = o_late[f, p - planes + SHIFT] if late else o_main[f, p]
    upper, lower = jnp.where(even, e, o), jnp.where(even, o, e)
    result = []
    for y in range(rows):
        where = pl.ds(y, tiles, stride=rows)
        value = partial[f, p, where, :]
        if y == rows - 1:
            value = value + (0.1 - 0.1 * flow[1, p, where, :]) * upper
        if y == 0:
            value = value + (0.1 + 0.1 * flow[1, p, where, :]) * lower
        result.append(value)
    return result


def glow_kernel(rows, total, partial, flow, gap, em, om, el, ol, thermal, glow):
    planes, height = partial.shape[1:3]
    tiles = height // rows
    halos = (em, om, el, ol)
    sums = [jnp.zeros((tiles, LANES), jnp.float32) for _ in range(rows)]
    for p in range(planes):
        light = finished(rows, GLOW, p, partial, flow, halos)
        heat = finished(rows, SPECIES, p, partial, flow, halos)
        for y in range(rows):
            where = pl.ds(y, tiles, stride=rows)
            gas = (1 - gap[p, where, :]).astype(jnp.float32)
            sums[y] += gas * light[y] * heat[y]
            thermal[p, where, :] = heat[y]
    for y in range(rows):
        glow[pl.ds(y, tiles, stride=rows), :] = sums[y] * (1.0 / total)


def final_kernel(rows, partial, flow, em, om, el, ol, out, stage, sems):
    planes, height = partial.shape[1:3]
    tiles = height // rows
    halos = (em, om, el, ol)
    copies = []
    for f in range(SPECIES):
        for p in range(planes):
            for y, value in enumerate(finished(rows, f, p, partial, flow, halos)):
                stage[f, p, pl.ds(y, tiles, stride=rows), :] = value
        copies.append(pltpu.make_async_copy(stage.at[f], out.at[f], sems.at[f]))
        copies[-1].start()
    for copy in copies:
        copy.wait()


def cost(us, size):
    return pl.CostEstimate(flops=int(us * 1e6), bytes_accessed=int(size), transcendentals=0)


def per_device(c, t, flow, gap, owner, rate, threshold, matrix, release, viewer):
    rows = t.shape[1]
    c, t, flow, gap = (tiled(x) for x in (c, t, flow, gap))
    planes, height, _ = t.shape
    tiles = height // rows
    f32 = functools.partial(jax.ShapeDtypeStruct, dtype=jnp.float32)
    count = lax.axis_size("ax")
    total = owner.shape[0]
    early = f32((FIELDS, planes - SHIFT, tiles, LANES))
    late = f32((FIELDS, SHIFT, tiles, LANES))
    ends = f32((FIELDS, SHIFT + 1, height, LANES))

    to_even, to_odd, up_even, up_odd = pl.pallas_call(
        functools.partial(send_kernel, rows),
        out_shape=(early, early, ends, ends),
        in_specs=[SMEM, VMEM, VMEM],
        out_specs=(VMEM,) * 4,
        compiler_params=pltpu.CompilerParams(vmem_limit_bytes=GRANT),
        name="send",
    )(owner, c, t)
    xs_even, xs_odd = swaps(lax.axis_size("xs"), 0), swaps(lax.axis_size("xs"), 1)
    ax_even, ax_odd = swaps(count, 0), swaps(count, 1)
    em = lax.ppermute(to_even, "xs", xs_even)
    om = lax.ppermute(to_odd, "xs", xs_odd)
    got_even = lax.ppermute(up_even, "ax", ax_even)
    got_odd = lax.ppermute(up_odd, "ax", ax_odd)
    late_even, late_odd = pl.pallas_call(
        functools.partial(late_kernel, rows),
        out_shape=(late, late),
        in_specs=[SMEM] + [VMEM] * 4,
        out_specs=(VMEM, VMEM),
        compiler_params=pltpu.CompilerParams(vmem_limit_bytes=GRANT),
        name="late",
    )(owner, c, t, got_even, got_odd)
    el = lax.ppermute(late_even, "xs", xs_even)
    ol = lax.ppermute(late_odd, "xs", xs_odd)
    partial = pl.pallas_call(
        functools.partial(main_kernel, rows),
        out_shape=f32((FIELDS, planes, height, LANES)),
        in_specs=[SMEM] * 5 + [VMEM] * 6,
        out_specs=VMEM,
        scratch_shapes=[pltpu.VMEM((FIELDS, planes + 2, height + 16, LANES), jnp.float32)],
        compiler_params=pltpu.CompilerParams(vmem_limit_bytes=GRANT),
        name="main",
    )(owner, rate, threshold, matrix, release, c, t, got_even, got_odd, flow, gap)
    thermal, glow = pl.pallas_call(
        functools.partial(glow_kernel, rows, total),
        out_shape=(f32((planes, height, LANES)), f32((height, LANES))),
        in_specs=[VMEM] * 7,
        out_specs=(VMEM, VMEM),
        compiler_params=pltpu.CompilerParams(vmem_limit_bytes=GRANT),
        name="glow",
    )(partial, flow, gap, em, om, el, ol)
    final = pl.pallas_call(
        functools.partial(final_kernel, rows),
        out_shape=f32((SPECIES, planes, height, LANES)),
        in_specs=[VMEM] * 6,
        out_specs=ANY,
        scratch_shapes=[
            pltpu.VMEM((SPECIES, planes, height, LANES), jnp.float32),
            pltpu.SemaphoreType.DMA((SPECIES,)),
        ],
        compiler_params=pltpu.CompilerParams(vmem_limit_bytes=GRANT),
        name="final",
    )(partial, flow, em, om, el, ol)
    place = lax.axis_index("ax")
    share = rows * (height // rows) // count
    if count in (2, 4) and tiles % count == 0:
        mine = lax.dynamic_slice_in_dim(glow, place * share, share, 0)
        for k in range(1, count):
            piece = lax.dynamic_slice_in_dim(glow, (place ^ k) * share, share, 0)
            mine += lax.ppermute(piece, "ax", [(i, i ^ k) for i in range(count)])
        error = untiled(mine - tiled(viewer), rows)
    else:
        picture = lax.psum(untiled(glow, rows), "ax")
        columns = picture.shape[1] // count
        mine = lax.dynamic_slice_in_dim(picture, place * columns, columns, 1)
        error = mine - viewer
    return untiled(final, rows), untiled(thermal, rows), error


def solution(mesh):
    volume, field = P(None, "ax", "xs", None), P("ax", "xs", None)
    in_specs = (volume, field, volume, field, P(), P(), P(), P(), P(), P("xs", "ax"))
    return jax.shard_map(
        per_device,
        mesh=mesh,
        in_specs=in_specs,
        out_specs=(volume, field, P("xs", "ax")),
        check_vma=False,
    )
```

```python
import functools

import jax
import jax.numpy as jnp
from jax import lax
from jax.experimental import pallas as pl
from jax.experimental.pallas import tpu as pltpu
from jax.sharding import PartitionSpec as P


SPECIES = 9
FIELDS = SPECIES + 1
GLOW = 4
SHIFT = 2
LANES = 128
GRANT = 16 << 20
FLOPS = 10**8


def tiled(x):
    *lead, rows, columns = x.shape
    n = len(lead)
    split = x.reshape(*lead, rows, columns // LANES, LANES)
    order = tuple(range(n)) + (n + 1, n, n + 2)
    return split.transpose(order).reshape(*lead, rows * columns // LANES, LANES)


def untiled(x, rows):
    *lead, height, _ = x.shape
    n = len(lead)
    split = x.reshape(*lead, height // rows, rows, LANES)
    order = tuple(range(n)) + (n + 1, n, n + 2)
    return split.transpose(order).reshape(*lead, rows, height // rows * LANES)


def swaps(count, offset):
    pairs = []
    for i in range(offset, count - 1, 2):
        pairs += [(i, i + 1), (i + 1, i)]
    return pairs


def remap_weights(owner, plane):
    total = owner.shape[0]
    inside = jnp.logical_and(plane >= 0, plane < total)
    hits = []
    for k in range(SHIFT + 1):
        p = plane + k
        mine = owner[jnp.clip(p, 0, total - 1)] == plane
        hits.append(jnp.where(inside & (p < total) & mine, 1.0, 0.0))
    count = hits[0] + hits[1] + hits[2]
    share = jnp.where(count > 2.5, 1.0 / 3.0, jnp.where(count > 1.5, 0.5, 1.0))
    kept = jnp.where(jnp.logical_and(inside, count < 0.5), 1.0, 0.0)
    return hits[0] * share + kept, hits[1] * share, hits[2] * share


def mix(weights, values):
    return weights[0] * values[0] + weights[1] * values[1] + weights[2] * values[2]


def old_field(c, t, f):
    return t if f == SPECIES else c.at[f]


def edge_starts(rows):
    even = lax.rem(lax.axis_index("xs"), 2) == 0
    return jnp.where(even, rows - 1, 0), jnp.where(even, 0, rows - 1)


def send_kernel(rows, c, t, owner, to_even, to_odd, up_even, up_odd, old, shares, table, sems):
    planes, height, _ = t.shape
    tiles = height // rows
    copies = [pltpu.make_async_copy(owner, table, sems.at[FIELDS])]
    for f in range(FIELDS):
        copies.append(pltpu.make_async_copy(old_field(c, t, f), old.at[f], sems.at[f]))
    for copy in copies:
        copy.start()
    copies[0].wait()
    first = lax.axis_index("ax") * planes
    weights = []
    for j in range(planes + 2):
        weights.append(remap_weights(table, first - 1 + j))
        for k, w in enumerate(weights[j]):
            shares[j, k] = jnp.full((8, LANES), w, jnp.float32)
    starts = edge_starts(rows)
    for f in range(FIELDS):
        copies[f + 1].wait()
        for start, out in zip(starts, (to_even, to_odd)):
            edge = [old[f, p, pl.ds(start, tiles, stride=rows), :] for p in range(planes)]
            for j in range(planes - SHIFT):
                out[f, j] = mix(weights[j + 1], edge[j : j + 3])
    even = lax.rem(lax.axis_index("ax"), 2) == 0
    depth = SHIFT + 1
    for f in range(FIELDS):
        up_even[f] = old[f, pl.ds(jnp.where(even, planes - depth, 0), depth)]
        up_odd[f] = old[f, pl.ds(jnp.where(even, 0, planes - depth), depth)]


def late_kernel(rows, shares, old, got_even, got_odd, to_even, to_odd):
    planes, height = old.shape[1:3]
    tiles = height // rows
    starts = edge_starts(rows)
    even = lax.rem(lax.axis_index("ax"), 2) == 0
    weights = [
        [shares[planes - SHIFT + 1 + j, k, :tiles] for k in range(SHIFT + 1)] for j in range(SHIFT)
    ]
    for f in range(FIELDS):
        for start, out in zip(starts, (to_even, to_odd)):
            where = pl.ds(start, tiles, stride=rows)
            edge = [old[f, planes - SHIFT + p, where, :] for p in range(SHIFT)]
            for p in range(SHIFT):
                edge.append(jnp.where(even, got_even[f, p, where, :], got_odd[f, p, where, :]))
            for j in range(SHIFT):
                out[f, j] = mix(weights[j], edge[j : j + 3])


def fetch(sources, targets, sems):
    copies = [
        pltpu.make_async_copy(source, target, sems.at[i])
        for i, (source, target) in enumerate(zip(sources, targets))
    ]
    for copy in copies:
        copy.start()
    return copies


def cells(rows, p, b, numbers, held, flow, gap, out):
    rate, threshold, matrix, release = numbers
    lane = lax.broadcasted_iota(jnp.int32, (8, LANES), 1)
    row = lax.rem(lax.broadcasted_iota(jnp.int32, (8, LANES), 0), rows)
    first_lane, last_lane = lane == 0, lane == LANES - 1
    here = pl.ds(8 * b, 8)
    va, vy, vz = (0.1 * flow[d, p, here] for d in range(3))
    up_y = jnp.where(row == rows - 1, 0.0, 0.1 - vy)
    low_y = jnp.where(row == 0, 0.0, 0.1 + vy)
    up_a, low_a, up_z, low_z = 0.1 - va, 0.1 + va, 0.1 - vz, 0.1 + vz

    def at(f, plane, offset):
        return held[f, plane, pl.ds(8 + 8 * b + offset, 8)]

    flux, mid = [], []
    for f in range(FIELDS):
        m = at(f, p + 1, 0)
        above_z = jnp.where(first_lane, at(f, p + 1, rows), m)
        below_z = jnp.where(last_lane, at(f, p + 1, -rows), m)
        flux.append(
            0.4 * m
            + up_a * at(f, p + 2, 0)
            + low_a * at(f, p, 0)
            + up_y * at(f, p + 1, 1)
            + low_y * at(f, p + 1, -1)
            + up_z * pltpu.roll(above_z, LANES - 1, 1)
            + low_z * pltpu.roll(below_z, 1, 1)
        )
        mid.append(m)
    inverse = 1.0 / mid[SPECIES]
    rates = []
    for r in range(SPECIES):
        speed = rate[r] * jnp.exp(-threshold[r] * inverse)
        rates.append(speed * mid[r] * mid[(r + 1) % SPECIES])
    half_gas = 0.5 * (1 - gap[p, here]).astype(jnp.float32)
    for f in range(FIELDS):
        parts = [
            (release[r] if f == SPECIES else matrix[f, r]) * rates[r] for r in range(SPECIES)
        ]
        out[f, p, here] = flux[f] + half_gas * sum(parts[1:], parts[0])


def inner_kernel(
    rows, shares, old, flow_in, gap_in, rate, threshold, matrix, release,
    held, out, flow, gap, s_rate, s_threshold, s_matrix, s_release, sems,
):
    planes, height = old.shape[1:3]
    numbers = (s_rate, s_threshold, s_matrix, s_release)
    copies = fetch(
        (flow_in, gap_in, rate, threshold, matrix, release), (flow, gap) + numbers, sems
    )
    zeros = jnp.zeros((8, LANES), jnp.float32)

    def remap(j, carry):
        for f in range(FIELDS):
            held[f, j + 1, 0:8] = zeros
            held[f, j + 1, 8 + height : 16 + height] = zeros
            for b in range(height // 8):
                held[f, j + 1, pl.ds(8 + 8 * b, 8)] = mix(
                    [shares[j + 1, k] for k in range(SHIFT + 1)],
                    [old[f, j + k, pl.ds(8 * b, 8)] for k in range(SHIFT + 1)],
                )
        return carry

    lax.fori_loop(0, planes - SHIFT, remap, 0)
    for copy in copies:
        copy.wait()

    def step(p, carry):
        for b in range(height // 8):
            cells(rows, p, b, numbers, held, flow, gap, out)
        return carry

    lax.fori_loop(1, planes - SHIFT - 1, step, 0)


def outer_kernel(
    rows, shares, old, got_even, got_odd, held_in, out_in, flow, gap, rate, threshold, matrix,
    release, held, out, s_rate, s_threshold, s_matrix, s_release, sems,
):
    planes, height = old.shape[1:3]
    numbers = (s_rate, s_threshold, s_matrix, s_release)
    copies = fetch((rate, threshold, matrix, release), numbers, sems)
    even = lax.rem(lax.axis_index("ax"), 2) == 0
    zeros = jnp.zeros((8, LANES), jnp.float32)

    def remap(f, carry):
        for j in range(planes - SHIFT, planes):
            held[f, j + 1, 0:8] = zeros
            held[f, j + 1, 8 + height : 16 + height] = zeros
        for b in range(height // 8):
            here, body = pl.ds(8 * b, 8), pl.ds(8 + 8 * b, 8)

            def pair(p, flip):
                one, two = got_even[f, p, here], got_odd[f, p, here]
                return jnp.where(even, two, one) if flip else jnp.where(even, one, two)

            def put(j, values):
                held[f, j + 1, body] = mix([shares[j + 1, k] for k in range(SHIFT + 1)], values)

            put(-1, [pair(SHIFT, True), old[f, 0, here], old[f, 1, here]])
            chain = [old[f, planes - SHIFT + p, here] for p in range(SHIFT)]
            chain += [pair(p, False) for p in range(SHIFT + 1)]
            for j in range(SHIFT + 1):
                put(planes - SHIFT + j, chain[j : j + 3])
        return carry

    lax.fori_loop(0, FIELDS, remap, 0)
    for copy in copies:
        copy.wait()

    def step(i, carry):
        p = jnp.where(i == 0, 0, planes - SHIFT - 2 + i)
        for b in range(height // 8):
            cells(rows, p, b, numbers, held, flow, gap, out)
        return carry

    lax.fori_loop(0, SHIFT + 2, step, 0)


def add_rows(rows, f, p, even, flow, one, two, out):
    tiles = one.shape[0]
    for y, sign, value in (
        (rows - 1, -0.1, jnp.where(even, one, two)),
        (0, 0.1, jnp.where(even, two, one)),
    ):
        where = pl.ds(y, tiles, stride=rows)
        out[f, p, where, :] = out[f, p, where, :] + (0.1 + sign * flow[1, p, where, :]) * value


def light(f_out, gap, p):
    gas = (1 - gap[p]).astype(jnp.float32)
    return gas * f_out[GLOW, p] * f_out[SPECIES, p]


def most_kernel(rows, part_in, flow, gap, one, two, part, final, thermal, glow, sems):
    planes, _ = part.shape[1:3]
    even = lax.rem(lax.axis_index("xs"), 2) == 0
    ready = planes - SHIFT
    order = [GLOW, SPECIES] + [f for f in range(SPECIES) if f != GLOW]
    copies = []
    for f in order:
        for p in range(ready):
            add_rows(rows, f, p, even, flow, one[f, p], two[f, p], part)
        target = thermal if f == SPECIES else final.at[f]
        here = pl.ds(0, ready)
        copies.append(pltpu.make_async_copy(part.at[f, here], target.at[here], sems.at[f]))
        copies[-1].start()
    total = light(part, gap, 0)
    for p in range(1, ready):
        total += light(part, gap, p)
    glow[...] = total
    for copy in copies:
        copy.wait()


def glow_kernel(rows, scale, part, flow, gap, one, two, glow, *rest):
    *outs, edge, picture = rest
    planes, height = part.shape[1:3]
    even = lax.rem(lax.axis_index("xs"), 2) == 0
    total = glow[...]
    for p in range(SHIFT):
        for i, f in enumerate((GLOW, SPECIES)):
            edge[i, p] = part[f, planes - SHIFT + p]
            tiles = one.shape[2]
            for y, sign, value in (
                (rows - 1, -0.1, jnp.where(even, one[f, p], two[f, p])),
                (0, 0.1, jnp.where(even, two[f, p], one[f, p])),
            ):
                where = pl.ds(y, tiles, stride=rows)
                slope = 0.1 + sign * flow[1, planes - SHIFT + p, where, :]
                edge[i, p, where, :] = edge[i, p, where, :] + slope * value
        gas = (1 - gap[planes - SHIFT + p]).astype(jnp.float32)
        total += gas * edge[0, p] * edge[1, p]
    picture[...] = total * scale
    split_rows(picture, outs, height, lax.axis_size("ax") // 2)


def split_rows(picture, outs, height, stage):
    if len(outs) == 1:
        outs[0][...] = picture[...]
        return
    half = height // 2
    upper = lax.rem(lax.axis_index("ax") // stage, 2)
    for keep, out in zip((upper, 1 - upper), outs):
        out[...] = picture[pl.ds(pl.multiple_of(keep * half, 8), half), :]


def join_kernel(stage, kept, got, *rest):
    *outs, picture = rest
    picture[...] = kept[...] + got[...]
    split_rows(picture, outs, picture.shape[0], stage)


def rest_kernel(rows, part_in, flow, one, two, final_in, thermal_in, part, final, thermal, sems):
    planes, _ = part.shape[1:3]
    even = lax.rem(lax.axis_index("xs"), 2) == 0
    here = pl.ds(planes - SHIFT, SHIFT)
    copies = []
    for f in range(FIELDS):
        for p in range(SHIFT):
            add_rows(rows, f, planes - SHIFT + p, even, flow, one[f, p], two[f, p], part)
        target = thermal if f == SPECIES else final.at[f]
        copies.append(pltpu.make_async_copy(part.at[f, here], target.at[here], sems.at[f]))
        copies[-1].start()
    for copy in copies:
        copy.wait()


def call(kernel, args, outs, scratch=(), aliases=None, us=1):
    spaces = {"v": pltpu.VMEM, "h": pltpu.HBM}
    return pl.pallas_call(
        kernel,
        out_shape=tuple(spaces[m](shape, jnp.float32) if m != "g" else jax.ShapeDtypeStruct(shape, jnp.int32) for shape, m in outs),
        in_specs=[pl.BlockSpec(memory_space=spaces[m]) for _, m in args],
        out_specs=tuple(pl.BlockSpec(memory_space=spaces.get(m, pltpu.VMEM)) for _, m in outs),
        scratch_shapes=list(scratch),
        input_output_aliases=aliases or {},
        cost_estimate=pl.CostEstimate(flops=int(us * FLOPS), bytes_accessed=0, transcendentals=0),
        compiler_params=pltpu.CompilerParams(vmem_limit_bytes=GRANT),
    )(*(pltpu.with_memory_space_constraint(a, spaces[m]) for a, m in args))


def per_device(c, t, flow, gap, owner, rate, threshold, matrix, release, viewer):
    rows = t.shape[1]
    c, t, flow, gap = (tiled(x) for x in (c, t, flow, gap))
    planes, height, _ = t.shape
    tiles = height // rows
    count = lax.axis_size("ax")
    early = ((FIELDS, planes - SHIFT, tiles, LANES), "v")
    late = ((FIELDS, SHIFT, tiles, LANES), "v")
    ends = ((FIELDS, SHIFT + 1, height, LANES), "v")
    whole = ((FIELDS, planes, height, LANES), "v")
    padded = ((FIELDS, planes + 2, height + 16, LANES), "v")
    numbers = [(x, "h") for x in (rate, threshold, matrix, release)]
    number_slots = [pltpu.SMEM(x.shape, x.dtype) for x, _ in numbers]
    sems = pltpu.SemaphoreType.DMA
    bind = functools.partial

    to_even, to_odd, up_even, up_odd, old, shares = call(
        bind(send_kernel, rows),
        [(c, "h"), (t, "h"), (owner, "h")],
        [early, early, ends, ends, whole, ((planes + 2, SHIFT + 1, 8, LANES), "v")],
        [pltpu.SMEM(owner.shape, owner.dtype), sems((FIELDS + 1,))],
    )
    xs_even, xs_odd = swaps(lax.axis_size("xs"), 0), swaps(lax.axis_size("xs"), 1)
    ax_even, ax_odd = swaps(count, 0), swaps(count, 1)
    em = lax.ppermute(to_even, "xs", xs_even)
    om = lax.ppermute(to_odd, "xs", xs_odd)
    got_even = lax.ppermute(up_even, "ax", ax_even)
    got_odd = lax.ppermute(up_odd, "ax", ax_odd)
    held, part, flow_v, gap_v = call(
        bind(inner_kernel, rows),
        [(shares, "v"), (old, "v"), (flow, "h"), (gap, "h")] + numbers,
        [padded, whole, (flow.shape, "v"), (gap.shape, "g")],
        number_slots + [sems((6,))], us=4,
    )
    late_even, late_odd = call(
        bind(late_kernel, rows),
        [(shares, "v"), (old, "v"), (got_even, "v"), (got_odd, "v")], [late, late],
    )
    el = lax.ppermute(late_even, "xs", xs_even)
    ol = lax.ppermute(late_odd, "xs", xs_odd)
    held, part = call(
        bind(outer_kernel, rows),
        [(shares, "v"), (old, "v"), (got_even, "v"), (got_odd, "v"), (held, "v"), (part, "v"),
         (flow_v, "v"), (gap_v, "v")] + numbers,
        [padded, whole], number_slots + [sems((4,))], {4: 0, 5: 1}, us=2,
    )
    final_shape = (SPECIES, planes, height, LANES)
    thermal_shape = (planes, height, LANES)
    part, final, thermal, glow = call(
        bind(most_kernel, rows),
        [(part, "v"), (flow_v, "v"), (gap_v, "v"), (em, "v"), (om, "v")],
        [whole, (final_shape, "h"), (thermal_shape, "h"), ((height, LANES), "v")],
        [sems((FIELDS,))], {0: 0}, us=2,
    )
    direct = count & (count - 1) == 0 and tiles % count == 0
    pieces = 2 if direct else 1
    glows = call(
        bind(glow_kernel, rows, 1.0 / owner.shape[0]),
        [(part, "v"), (flow_v, "v"), (gap_v, "v"), (el, "v"), (ol, "v"), (glow, "v")],
        [((height // pieces, LANES), "v")] * pieces,
        [pltpu.VMEM((2, SHIFT, height, LANES), jnp.float32), pltpu.VMEM((height, LANES), jnp.float32)],
    )
    part, final, thermal = call(
        bind(rest_kernel, rows),
        [(part, "v"), (flow_v, "v"), (el, "v"), (ol, "v"), (final, "h"), (thermal, "h")],
        [whole, (final_shape, "h"), (thermal_shape, "h")],
        [sems((FIELDS,))], {0: 0, 4: 1, 5: 2},
    )
    place = lax.axis_index("ax")
    if direct:
        stage = count // 2
        while True:
            pairs = [(i, i ^ stage) for i in range(count)]
            kept, got = glows[0], lax.ppermute(glows[1], "ax", pairs)
            if stage == 1:
                break
            stage //= 2
            size = kept.shape[0]
            glows = call(
                bind(join_kernel, stage), [(kept, "v"), (got, "v")],
                [((size // 2, LANES), "v")] * 2, [pltpu.VMEM((size, LANES), jnp.float32)],
            )
        error = untiled(kept + got - tiled(viewer), rows)
    else:
        picture = lax.psum(untiled(glows[0], rows), "ax")
        columns = picture.shape[1] // count
        mine = lax.dynamic_slice_in_dim(picture, place * columns, columns, 1)
        error = mine - viewer
    return untiled(final, rows), untiled(thermal, rows), error


def solution(mesh):
    volume, field = P(None, "ax", "xs", None), P("ax", "xs", None)
    in_specs = (volume, field, volume, field, P(), P(), P(), P(), P(), P("xs", "ax"))
    return jax.shard_map(
        per_device,
        mesh=mesh,
        in_specs=in_specs,
        out_specs=(volume, field, P("xs", "ax")),
        check_vma=False,
    )
```

```python
import functools

import jax
import jax.numpy as jnp
from jax import lax
from jax.experimental import pallas as pl
from jax.experimental.pallas import tpu as pltpu
from jax.sharding import PartitionSpec as P


SPECIES = 9
FIELDS = SPECIES + 1
GLOW = 4
ORDER = (GLOW, SPECIES) + tuple(f for f in range(SPECIES) if f != GLOW)
EARLY = 5
SHIFT = 2
LANES = 128
GRANT = 16 << 20
FLOPS = 10**8


def tiled(x):
    *lead, rows, columns = x.shape
    n = len(lead)
    split = x.reshape(*lead, rows, columns // LANES, LANES)
    order = tuple(range(n)) + (n + 1, n, n + 2)
    return split.transpose(order).reshape(*lead, rows * columns // LANES, LANES)


def untiled(x, rows):
    *lead, height, _ = x.shape
    n = len(lead)
    split = x.reshape(*lead, height // rows, rows, LANES)
    order = tuple(range(n)) + (n + 1, n, n + 2)
    return split.transpose(order).reshape(*lead, rows, height // rows * LANES)


def swaps(slabs, count, offset):
    pairs = []
    for slab in range(slabs):
        alone = set(range(count))
        for i in range(offset, count - 1, 2):
            pairs += [(slab * count + i, slab * count + i + 1)]
            pairs += [(slab * count + i + 1, slab * count + i)]
            alone -= {i, i + 1}
        if slabs % 2 == 0:
            pairs += [(slab * count + i, (slab ^ 1) * count + i) for i in sorted(alone)]
    return pairs


def ring(count, distance):
    return [(i, (i + distance) % count) for i in range(count)]


def remap_weights(owner, plane):
    total = owner.shape[0]
    inside = jnp.logical_and(plane >= 0, plane < total)
    hits = []
    for k in range(SHIFT + 1):
        p = plane + k
        mine = owner[jnp.clip(p, 0, total - 1)] == plane
        hits.append(jnp.where(inside & (p < total) & mine, 1.0, 0.0))
    count = hits[0] + hits[1] + hits[2]
    share = jnp.where(count > 2.5, 1.0 / 3.0, jnp.where(count > 1.5, 0.5, 1.0))
    kept = jnp.where(jnp.logical_and(inside, count < 0.5), 1.0, 0.0)
    return hits[0] * share + kept, hits[1] * share, hits[2] * share


def mix(weights, values):
    return weights[0] * values[0] + weights[1] * values[1] + weights[2] * values[2]


def old_field(c, t, f):
    return t if f == SPECIES else c.at[f]


def edge_starts(rows):
    even = lax.rem(lax.axis_index("xs"), 2) == 0
    return jnp.where(even, rows - 1, 0), jnp.where(even, 0, rows - 1)


def rows_sent(planes):
    ready = planes - SHIFT
    ends = range(ready, planes)
    first = [(f, p) for f in ORDER[:EARLY] for p in range(ready)]
    middle = [(f, p) for f in ORDER[:2] for p in ends]
    last = [(f, p) for f in ORDER[EARLY:] for p in range(ready)]
    last_late = [(f, p) for f in ORDER[2:] for p in ends]
    return first, middle, last, last_late


def load_fields(c, t, fields, old, sems):
    copies = {}
    for f in fields:
        copies[f] = pltpu.make_async_copy(old_field(c, t, f), old.at[f], sems.at[f])
        copies[f].start()
    return copies


def edge_rows(rows, f, listed, old, weights, outs):
    planes, height = old.shape[1:3]
    tiles = height // rows
    for start, out in zip(edge_starts(rows), outs):
        edge = [old[f, p, pl.ds(start, tiles, stride=rows), :] for p in range(planes)]
        for j in range(planes - SHIFT):
            out[listed.index((f, j))] = mix(weights[j + 1], edge[j : j + 3])


def send_kernel(rows, c, t, owner, to_even, to_odd, old, shares, table, sems):
    planes = t.shape[0]
    wanted = pltpu.make_async_copy(owner, table, sems.at[FIELDS])
    wanted.start()
    copies = load_fields(c, t, ORDER[:EARLY], old, sems)
    wanted.wait()
    first = lax.axis_index("ax") * planes
    weights = []
    for j in range(planes + 2):
        weights.append(remap_weights(table, first - 1 + j))
        for k, w in enumerate(weights[j]):
            shares[j, k] = jnp.full((8, LANES), w, jnp.float32)
    for f in ORDER[:EARLY]:
        copies[f].wait()
        edge_rows(rows, f, rows_sent(planes)[0], old, weights, (to_even, to_odd))


def more_kernel(
    rows, c, t, shares, old_in, last_even, last_odd, lips, up, down, old, sems,
):
    planes, height, _ = t.shape
    tiles = height // rows
    copies = load_fields(c, t, ORDER[EARLY:], old, sems)
    weights = [[shares[j, k, :tiles] for k in range(SHIFT + 1)] for j in range(planes + 2)]
    for f in ORDER:
        if f in copies:
            copies[f].wait()
            edge_rows(rows, f, rows_sent(planes)[2], old, weights, (last_even, last_odd))
        up[f] = old[f, 0 : SHIFT + 1]
        for p in range(SHIFT):
            for i, y in enumerate((0, rows - 1)):
                lips[(f * SHIFT + p) * 2 + i] = old[f, p, pl.ds(y, tiles, stride=rows), :]
        down[f] = old[f, planes - 1]


def late_kernel(
    rows, shares, old, lips, last_even_in, last_odd_in, to_even, to_odd, last_even, last_odd,
):
    planes, height = old.shape[1:3]
    tiles = height // rows
    starts = edge_starts(rows)
    weights = [
        [shares[planes - SHIFT + 1 + j, k, :tiles] for k in range(SHIFT + 1)] for j in range(SHIFT)
    ]
    _, middle, last, last_late = rows_sent(planes)
    for f in range(FIELDS):
        glows = f in ORDER[:2]
        listed = middle if glows else last + last_late
        for start, out in zip(starts, (to_even, to_odd) if glows else (last_even, last_odd)):
            where = pl.ds(start, tiles, stride=rows)
            edge = [old[f, planes - SHIFT + p, where, :] for p in range(SHIFT)]
            for p in range(SHIFT):
                low, high = (lips[(f * SHIFT + p) * 2 + i] for i in range(2))
                edge.append(jnp.where(start == 0, low, high))
            for j in range(SHIFT):
                out[listed.index((f, planes - SHIFT + j))] = mix(weights[j], edge[j : j + 3])


def fetch(sources, targets, sems):
    copies = [
        pltpu.make_async_copy(source, target, sems.at[i])
        for i, (source, target) in enumerate(zip(sources, targets))
    ]
    for copy in copies:
        copy.start()
    return copies


def cells(rows, p, b, numbers, held, flow, gap, out):
    rate, threshold, matrix, release = numbers
    lane = lax.broadcasted_iota(jnp.int32, (8, LANES), 1)
    row = lax.rem(lax.broadcasted_iota(jnp.int32, (8, LANES), 0), rows)
    first_lane, last_lane = lane == 0, lane == LANES - 1
    here = pl.ds(8 * b, 8)
    va, vy, vz = (0.1 * flow[d, p, here] for d in range(3))
    up_y = jnp.where(row == rows - 1, 0.0, 0.1 - vy)
    low_y = jnp.where(row == 0, 0.0, 0.1 + vy)
    up_a, low_a, up_z, low_z = 0.1 - va, 0.1 + va, 0.1 - vz, 0.1 + vz

    def at(f, plane, offset):
        return held[f, plane, pl.ds(8 + 8 * b + offset, 8)]

    flux, mid = [], []
    for f in range(FIELDS):
        m = at(f, p + 1, 0)
        above_z = jnp.where(first_lane, at(f, p + 1, rows), m)
        below_z = jnp.where(last_lane, at(f, p + 1, -rows), m)
        flux.append(
            0.4 * m
            + up_a * at(f, p + 2, 0)
            + low_a * at(f, p, 0)
            + up_y * at(f, p + 1, 1)
            + low_y * at(f, p + 1, -1)
            + up_z * pltpu.roll(above_z, LANES - 1, 1)
            + low_z * pltpu.roll(below_z, 1, 1)
        )
        mid.append(m)
    inverse = 1.0 / mid[SPECIES]
    rates = []
    for r in range(SPECIES):
        speed = rate[r] * jnp.exp(-threshold[r] * inverse)
        rates.append(speed * mid[r] * mid[(r + 1) % SPECIES])
    half_gas = 0.5 * (1 - gap[p, here]).astype(jnp.float32)
    for f in range(FIELDS):
        parts = [
            (release[r] if f == SPECIES else matrix[f, r]) * rates[r] for r in range(SPECIES)
        ]
        out[f, p, here] = flux[f] + half_gas * sum(parts[1:], parts[0])


def inner_kernel(
    rows, shares, old, flow_in, gap_in, rate, threshold, matrix, release,
    held, out, flow, gap, s_rate, s_threshold, s_matrix, s_release, sems,
):
    planes, height = old.shape[1:3]
    numbers = (s_rate, s_threshold, s_matrix, s_release)
    copies = fetch(
        (flow_in, gap_in, rate, threshold, matrix, release), (flow, gap) + numbers, sems
    )
    zeros = jnp.zeros((8, LANES), jnp.float32)

    def remap(j, carry):
        for f in range(FIELDS):
            held[f, j + 1, 0:8] = zeros
            held[f, j + 1, 8 + height : 16 + height] = zeros
            for b in range(height // 8):
                held[f, j + 1, pl.ds(8 + 8 * b, 8)] = mix(
                    [shares[j + 1, k] for k in range(SHIFT + 1)],
                    [old[f, j + k, pl.ds(8 * b, 8)] for k in range(SHIFT + 1)],
                )
        return carry

    lax.fori_loop(0, planes - SHIFT, remap, 0)
    for f in range(FIELDS):
        for b in range(height // 8):
            for j in (0, planes - SHIFT + 1):
                held[f, j, pl.ds(8 + 8 * b, 8)] = zeros
    for copy in copies:
        copy.wait()

    def step(p, carry):
        for b in range(height // 8):
            cells(rows, p, b, numbers, held, flow, gap, out)
        return carry

    lax.fori_loop(0, planes - SHIFT, step, 0)


def outer_kernel(
    rows, shares, old, upper, lower, held_in, out_in, flow, gap, rate, threshold, matrix,
    release, held, out, s_rate, s_threshold, s_matrix, s_release, sems,
):
    planes, height = old.shape[1:3]
    numbers = (s_rate, s_threshold, s_matrix, s_release)
    copies = fetch((rate, threshold, matrix, release), numbers, sems)
    zeros = jnp.zeros((8, LANES), jnp.float32)

    def remap(f, carry):
        for j in range(planes - SHIFT, planes):
            held[f, j + 1, 0:8] = zeros
            held[f, j + 1, 8 + height : 16 + height] = zeros
        for b in range(height // 8):
            here, body = pl.ds(8 * b, 8), pl.ds(8 + 8 * b, 8)

            def put(j, values):
                held[f, j + 1, body] = mix([shares[j + 1, k] for k in range(SHIFT + 1)], values)

            put(-1, [lower[f, here], old[f, 0, here], old[f, 1, here]])
            chain = [old[f, planes - SHIFT + p, here] for p in range(SHIFT)]
            chain += [upper[f, p, here] for p in range(SHIFT + 1)]
            for j in range(SHIFT + 1):
                put(planes - SHIFT + j, chain[j : j + 3])
        return carry

    lax.fori_loop(0, FIELDS, remap, 0)
    for copy in copies:
        copy.wait()

    for b in range(height // 8):
        here, body = pl.ds(8 * b, 8), pl.ds(8 + 8 * b, 8)
        for p, j, sign in ((0, 0, 0.1), (planes - SHIFT - 1, planes - SHIFT + 1, -0.1)):
            slope = 0.1 + sign * flow[0, p, here]
            for f in range(FIELDS):
                out[f, p, here] = out[f, p, here] + slope * held[f, j, body]

    def step(p, carry):
        for b in range(height // 8):
            cells(rows, p, b, numbers, held, flow, gap, out)
        return carry

    lax.fori_loop(planes - SHIFT, planes, step, 0)


def add_rows(rows, f, p, sides, flow, one, two, i, out):
    tiles = one.shape[1]
    even, low, high = sides
    for y, keep, sign, value in (
        (rows - 1, high, -1.0, jnp.where(even, one[i], two[i])),
        (0, low, 1.0, jnp.where(even, two[i], one[i])),
    ):
        where = pl.ds(y, tiles, stride=rows)
        slope = keep + (sign * keep) * flow[1, p, where, :]
        out[f, p, where, :] = out[f, p, where, :] + slope * value


def sides_of():
    place = lax.axis_index("xs")
    low = jnp.where(place > 0, 0.1, 0.0)
    high = jnp.where(place < lax.axis_size("xs") - 1, 0.1, 0.0)
    return lax.rem(place, 2) == 0, low, high


def glow_kernel(rows, scale, part_in, flow, gap, e1, o1, e2, o2, part, *rest):
    *outs, picture = rest
    planes, height = part.shape[1:3]
    sides = sides_of()
    first, middle, _, _ = rows_sent(planes)
    for listed, one, two in ((first[: 2 * (planes - SHIFT)], e1, o1), (middle, e2, o2)):
        for i, (f, p) in enumerate(listed):
            add_rows(rows, f, p, sides, flow, one, two, i, part)
    for b in range(height // 8):
        here = pl.ds(8 * b, 8)
        total = jnp.zeros((8, LANES), jnp.float32)
        for p in range(planes):
            gas = (1 - gap[p, here]).astype(jnp.float32)
            total += gas * part[GLOW, p, here] * part[SPECIES, p, here]
        picture[here, :] = total * scale
    split_rows(picture, outs, height, lax.axis_size("ax") // 2)


def error_kernel(kept, got, viewer, out, stage, sem):
    stage[...] = kept[...] + got[...] - viewer[...]
    copy = pltpu.make_async_copy(stage, out, sem)
    copy.start()
    copy.wait()


def store_kernel(rows, last, part_in, flow, one, two, *rest):
    part, final, thermal, sems = rest[-4:]
    planes, _ = part.shape[1:3]
    sides = sides_of()
    ready = planes - SHIFT
    now, _, late, late_ends = rows_sent(planes)
    listed = late + late_ends if last else now
    ends, most, everything = pl.ds(ready, SHIFT), pl.ds(0, ready), pl.ds(0, planes)
    if last:
        done = [(f, everything) for f in ORDER[EARLY:]] + [(f, ends) for f in ORDER[2:EARLY]]
    else:
        done = [(f, everything) for f in ORDER[:2]] + [(f, most) for f in ORDER[2:EARLY]]
    copies = []
    for n, (f, span) in enumerate(done):
        for i, (field, p) in enumerate(listed):
            if field == f and f not in ORDER[:2]:
                add_rows(rows, f, p, sides, flow, one, two, i, part)
        target = thermal if f == SPECIES else final.at[f]
        copies.append(pltpu.make_async_copy(part.at[f, span], target.at[span], sems.at[n]))
        copies[-1].start()
    for copy in copies:
        copy.wait()


def split_rows(picture, outs, height, stage):
    if len(outs) == 1:
        outs[0][...] = picture[...]
        return
    half = height // 2
    upper = lax.rem(lax.axis_index("ax") // stage, 2)
    for keep, out in zip((upper, 1 - upper), outs):
        out[...] = picture[pl.ds(pl.multiple_of(keep * half, 8), half), :]


def join_kernel(stage, kept, got, *rest):
    *outs, picture = rest
    picture[...] = kept[...] + got[...]
    split_rows(picture, outs, picture.shape[0], stage)


def call(kernel, args, outs, scratch=(), aliases=None, us=1):
    spaces = {"v": pltpu.VMEM, "h": pltpu.HBM}
    return pl.pallas_call(
        kernel,
        out_shape=tuple(spaces[m](shape, jnp.float32) if m != "g" else jax.ShapeDtypeStruct(shape, jnp.int32) for shape, m in outs),
        in_specs=[pl.BlockSpec(memory_space=spaces[m]) for _, m in args],
        out_specs=tuple(pl.BlockSpec(memory_space=spaces.get(m, pltpu.VMEM)) for _, m in outs),
        scratch_shapes=list(scratch),
        input_output_aliases=aliases or {},
        cost_estimate=pl.CostEstimate(flops=int(us * FLOPS), bytes_accessed=0, transcendentals=0),
        compiler_params=pltpu.CompilerParams(vmem_limit_bytes=GRANT),
    )(*(pltpu.with_memory_space_constraint(a, spaces[m]) for a, m in args))


def per_device(c, t, flow, gap, owner, rate, threshold, matrix, release, viewer):
    rows = t.shape[1]
    c, t, flow, gap = (tiled(x) for x in (c, t, flow, gap))
    planes, height, _ = t.shape
    tiles = height // rows
    count = lax.axis_size("ax")
    first, middle, last, last_late = rows_sent(planes)
    first, middle, last = (
        ((len(x), tiles, LANES), "v") for x in (first, middle, last + last_late)
    )
    ends = ((FIELDS, SHIFT + 1, height, LANES), "v")
    whole = ((FIELDS, planes, height, LANES), "v")
    padded = ((FIELDS, planes + 2, height + 16, LANES), "v")
    numbers = [(x, "h") for x in (rate, threshold, matrix, release)]
    number_slots = [pltpu.SMEM(x.shape, x.dtype) for x, _ in numbers]
    sems = pltpu.SemaphoreType.DMA
    bind = functools.partial

    to_even, to_odd, old, shares = call(
        bind(send_kernel, rows), [(c, "h"), (t, "h"), (owner, "h")],
        [first, first, whole, ((planes + 2, SHIFT + 1, 8, LANES), "v")],
        [pltpu.SMEM(owner.shape, owner.dtype), sems((FIELDS + 1,))],
    )
    last_even, last_odd, lips, up, down, old = call(
        bind(more_kernel, rows), [(c, "h"), (t, "h"), (shares, "v"), (old, "v")],
        [last, last, ((FIELDS * SHIFT * 2, tiles, LANES), "v"), ends,
         ((FIELDS, height, LANES), "v"), whole],
        [sems((FIELDS,))], {3: 5},
    )
    tiling = lax.axis_size("xs")
    xs_even, xs_odd = swaps(count, tiling, 0), swaps(count, tiling, 1)
    lips = lax.ppermute(lips, "ax", ring(count, -1))
    upper = lax.ppermute(up, "ax", ring(count, -1))
    e1 = lax.ppermute(to_even, ("ax", "xs"), xs_even)
    o1 = lax.ppermute(to_odd, ("ax", "xs"), xs_odd)
    lower = lax.ppermute(down, "ax", ring(count, 1))
    held, part, flow_v, gap_v = call(
        bind(inner_kernel, rows),
        [(shares, "v"), (old, "v"), (flow, "h"), (gap, "h")] + numbers,
        [padded, whole, (flow.shape, "v"), (gap.shape, "g")],
        number_slots + [sems((6,))], us=4,
    )
    late_even, late_odd, last_even, last_odd = call(
        bind(late_kernel, rows),
        [(shares, "v"), (old, "v"), (lips, "v"), (last_even, "v"), (last_odd, "v")],
        [middle, middle, last, last], (), {3: 2, 4: 3},
    )
    e2 = lax.ppermute(late_even, ("ax", "xs"), xs_even)
    o2 = lax.ppermute(late_odd, ("ax", "xs"), xs_odd)
    e3 = lax.ppermute(last_even, ("ax", "xs"), xs_even)
    o3 = lax.ppermute(last_odd, ("ax", "xs"), xs_odd)
    held, part = call(
        bind(outer_kernel, rows),
        [(shares, "v"), (old, "v"), (upper, "v"), (lower, "v"), (held, "v"), (part, "v"),
         (flow_v, "v"), (gap_v, "v")] + numbers,
        [padded, whole], number_slots + [sems((4,))], {4: 0, 5: 1}, us=2,
    )
    final_shape = (SPECIES, planes, height, LANES)
    thermal_shape = (planes, height, LANES)
    direct = count & (count - 1) == 0 and tiles % count == 0
    pieces = 2 if direct else 1
    part, *glows = call(
        bind(glow_kernel, rows, 1.0 / owner.shape[0]),
        [(part, "v"), (flow_v, "v"), (gap_v, "v"), (e1, "v"), (o1, "v"), (e2, "v"), (o2, "v")],
        [whole] + [((height // pieces, LANES), "v")] * pieces,
        [pltpu.VMEM((height, LANES), jnp.float32)], {0: 0},
    )
    stores = [whole, (final_shape, "h"), (thermal_shape, "h")]
    part, final, thermal = call(
        bind(store_kernel, rows, False),
        [(part, "v"), (flow_v, "v"), (e1, "v"), (o1, "v")],
        stores, [sems((FIELDS,))], {0: 0},
    )
    part, final, thermal = call(
        bind(store_kernel, rows, True),
        [(part, "v"), (flow_v, "v"), (e3, "v"), (o3, "v"), (final, "h"), (thermal, "h")],
        stores, [sems((FIELDS,))], {0: 0, 4: 1, 5: 2},
    )
    place = lax.axis_index("ax")
    if direct:
        stage = count // 2
        while True:
            pairs = [(i, i ^ stage) for i in range(count)]
            kept, got = glows[0], lax.ppermute(glows[1], "ax", pairs)
            if stage == 1:
                break
            stage //= 2
            size = kept.shape[0]
            glows = call(
                bind(join_kernel, stage), [(kept, "v"), (got, "v")],
                [((size // 2, LANES), "v")] * 2, [pltpu.VMEM((size, LANES), jnp.float32)],
            )
        (error,) = call(
            error_kernel, [(kept, "v"), (got, "v"), (tiled(viewer), "v")],
            [(kept.shape, "h")], [pltpu.VMEM(kept.shape, jnp.float32), sems],
        )
        error = untiled(error, rows)
    else:
        picture = lax.psum(untiled(glows[0], rows), "ax")
        columns = picture.shape[1] // count
        mine = lax.dynamic_slice_in_dim(picture, place * columns, columns, 1)
        error = mine - viewer
    return untiled(final, rows), untiled(thermal, rows), error


def solution(mesh):
    volume, field = P(None, "ax", "xs", None), P("ax", "xs", None)
    in_specs = (volume, field, volume, field, P(), P(), P(), P(), P(), P("xs", "ax"))
    return jax.shard_map(
        per_device,
        mesh=mesh,
        in_specs=in_specs,
        out_specs=(volume, field, P("xs", "ax")),
        check_vma=False,
    )
```

```python
import functools

import jax
import jax.numpy as jnp
from jax import lax
from jax.experimental import pallas as pl
from jax.experimental.pallas import tpu as pltpu
from jax.sharding import PartitionSpec as P


SPECIES = 9
FIELDS = SPECIES + 1
GLOW = 4
ORDER = (GLOW, SPECIES) + tuple(f for f in range(SPECIES) if f != GLOW)
EARLY = 6
HEAD = 4
SHIFT = 2
LANES = 128
GRANT = 16 << 20
FLOPS = 10**8


def tiled(x):
    *lead, rows, columns = x.shape
    n = len(lead)
    split = x.reshape(*lead, rows, columns // LANES, LANES)
    order = tuple(range(n)) + (n + 1, n, n + 2)
    return split.transpose(order).reshape(*lead, rows * columns // LANES, LANES)


def untiled(x, rows):
    *lead, height, _ = x.shape
    n = len(lead)
    split = x.reshape(*lead, height // rows, rows, LANES)
    order = tuple(range(n)) + (n + 1, n, n + 2)
    return split.transpose(order).reshape(*lead, rows, height // rows * LANES)


def swaps(slabs, count, offset):
    pairs = []
    for slab in range(slabs):
        alone = set(range(count))
        for i in range(offset, count - 1, 2):
            pairs += [(slab * count + i, slab * count + i + 1)]
            pairs += [(slab * count + i + 1, slab * count + i)]
            alone -= {i, i + 1}
        if slabs % 2 == 0:
            pairs += [(slab * count + i, (slab ^ 1) * count + i) for i in sorted(alone)]
    return pairs


def ring(count, distance):
    return [(i, (i + distance) % count) for i in range(count)]


def remap_weights(owner, first, count):
    total = owner.shape[0]
    landed = []
    for p in range(count + SHIFT):
        there = owner[jnp.clip(first + p, 0, total - 1)]
        landed.append(jnp.where(first + p < total, there, -1))
    result = []
    for j in range(count):
        plane = first + j
        hits = [landed[j + k] == plane for k in range(SHIFT + 1)]
        number = sum(jnp.where(hit, 1, 0) for hit in hits)
        share = jnp.where(number == 3, 1.0 / 3.0, jnp.where(number == 2, 0.5, 1.0))
        share = jnp.where(jnp.logical_and(plane >= 0, plane < total), share, 0.0)
        hits[0] = jnp.logical_or(hits[0], number == 0)
        result.append([jnp.where(hit, share, 0.0) for hit in hits])
    return result


def mix(weights, values):
    return weights[0] * values[0] + weights[1] * values[1] + weights[2] * values[2]


def old_field(c, t, f):
    return t if f == SPECIES else c.at[f]


def edge_starts(rows):
    even = lax.rem(lax.axis_index("xs"), 2) == 0
    return jnp.where(even, rows - 1, 0), jnp.where(even, 0, rows - 1)


def rows_sent(planes):
    ready = planes - SHIFT
    ends = range(ready, planes)
    first = [(f, p) for f in ORDER[:EARLY] for p in range(ready)]
    middle = [(f, p) for f in ORDER[:2] for p in ends]
    last = [(f, p) for f in ORDER[EARLY:] for p in range(ready)]
    last_late = [(f, p) for f in ORDER[2:] for p in ends]
    return first, middle, last, last_late


def load_fields(c, t, fields, old, sems):
    copies = {}
    for f in fields:
        copies[f] = pltpu.make_async_copy(old_field(c, t, f), old.at[f], sems.at[f])
        copies[f].start()
    return copies


def edge_rows(rows, f, start, listed, old, weights, out):
    planes, height = old.shape[1:3]
    tiles = height // rows
    edge = [old[f, p, pl.ds(start, tiles, stride=rows), :] for p in range(planes)]
    for j in range(planes - SHIFT):
        out[listed.index((f, j))] = mix(weights[j + 1], edge[j : j + 3])


def send_kernel(rows, c, t, owner, to_even, shares, table, edge, sems):
    planes = t.shape[0]
    tiles = t.shape[2] // LANES
    wanted = pltpu.make_async_copy(owner, table, sems.at[FIELDS])
    wanted.start()
    start = edge_starts(rows)[0]
    copies = []
    for i, f in enumerate(ORDER[:EARLY]):
        source = old_field(c, t, f).at[:, pl.ds(start, 1), :]
        copies.append(pltpu.make_async_copy(source, edge.at[i], sems.at[f]))
        copies[-1].start()
    wanted.wait()
    first = lax.axis_index("ax") * planes
    weights = remap_weights(table, first - 1, planes + 2)
    for j, triple in enumerate(weights):
        for k, w in enumerate(triple):
            shares[j, k] = jnp.full((8, LANES), w, jnp.float32)
    listed = rows_sent(planes)[0]
    for i, f in enumerate(ORDER[:EARLY]):
        copies[i].wait()
        for j in range(planes - SHIFT):
            to_even[listed.index((f, j))] = mix(
                weights[j + 1], [edge[i, j + k].reshape(tiles, LANES) for k in range(SHIFT + 1)]
            )


def more_kernel(
    rows, c, t, shares, to_odd, last_even, last_odd, lips, up, down, old, sems,
):
    planes, height, _ = t.shape
    tiles = height // rows
    copies = load_fields(c, t, ORDER, old, sems)
    weights = [[shares[j, k, :tiles] for k in range(SHIFT + 1)] for j in range(planes + 2)]
    even_start, odd_start = edge_starts(rows)
    first, _, last, _ = rows_sent(planes)
    for f in ORDER:
        copies[f].wait()
        if f in ORDER[EARLY:]:
            edge_rows(rows, f, even_start, last, old, weights, last_even)
            edge_rows(rows, f, odd_start, last, old, weights, last_odd)
        else:
            edge_rows(rows, f, odd_start, first, old, weights, to_odd)
        up[f] = old[f, 0 : SHIFT + 1]
        for p in range(SHIFT):
            for i, y in enumerate((0, rows - 1)):
                lips[(f * SHIFT + p) * 2 + i] = old[f, p, pl.ds(y, tiles, stride=rows), :]
        down[f] = old[f, planes - 1]


def late_kernel(
    rows, shares, old, lips, last_even_in, last_odd_in, to_even, to_odd, last_even, last_odd,
):
    planes, height = old.shape[1:3]
    tiles = height // rows
    starts = edge_starts(rows)
    weights = [
        [shares[planes - SHIFT + 1 + j, k, :tiles] for k in range(SHIFT + 1)] for j in range(SHIFT)
    ]
    _, middle, last, last_late = rows_sent(planes)
    for f in range(FIELDS):
        glows = f in ORDER[:2]
        listed = middle if glows else last + last_late
        for start, out in zip(starts, (to_even, to_odd) if glows else (last_even, last_odd)):
            where = pl.ds(start, tiles, stride=rows)
            edge = [old[f, planes - SHIFT + p, where, :] for p in range(SHIFT)]
            for p in range(SHIFT):
                low, high = (lips[(f * SHIFT + p) * 2 + i] for i in range(2))
                edge.append(jnp.where(start == 0, low, high))
            for j in range(SHIFT):
                out[listed.index((f, planes - SHIFT + j))] = mix(weights[j], edge[j : j + 3])


def fetch(sources, targets, sems):
    copies = [
        pltpu.make_async_copy(source, target, sems.at[i])
        for i, (source, target) in enumerate(zip(sources, targets))
    ]
    for copy in copies:
        copy.start()
    return copies


def cells(rows, p, b, numbers, held, flow, gap, out):
    rate, threshold, matrix, release = numbers
    lane = lax.broadcasted_iota(jnp.int32, (8, LANES), 1)
    row = lax.rem(lax.broadcasted_iota(jnp.int32, (8, LANES), 0), rows)
    first_lane, last_lane = lane == 0, lane == LANES - 1
    here = pl.ds(8 * b, 8)
    va, vy, vz = (0.1 * flow[d, p, here] for d in range(3))
    up_y = jnp.where(row == rows - 1, 0.0, 0.1 - vy)
    low_y = jnp.where(row == 0, 0.0, 0.1 + vy)
    up_a, low_a, up_z, low_z = 0.1 - va, 0.1 + va, 0.1 - vz, 0.1 + vz

    def at(f, plane, offset):
        return held[f, plane, pl.ds(8 + 8 * b + offset, 8)]

    flux, mid = [], []
    for f in range(FIELDS):
        m = at(f, p + 1, 0)
        above_z = jnp.where(first_lane, at(f, p + 1, rows), m)
        below_z = jnp.where(last_lane, at(f, p + 1, -rows), m)
        flux.append(
            0.4 * m
            + up_a * at(f, p + 2, 0)
            + low_a * at(f, p, 0)
            + up_y * at(f, p + 1, 1)
            + low_y * at(f, p + 1, -1)
            + up_z * pltpu.roll(above_z, LANES - 1, 1)
            + low_z * pltpu.roll(below_z, 1, 1)
        )
        mid.append(m)
    inverse = 1.0 / mid[SPECIES]
    rates = []
    for r in range(SPECIES):
        speed = rate[r] * jnp.exp(-threshold[r] * inverse)
        rates.append(speed * mid[r] * mid[(r + 1) % SPECIES])
    half_gas = 0.5 * (1 - gap[p, here]).astype(jnp.float32)
    for f in range(FIELDS):
        parts = [
            (release[r] if f == SPECIES else matrix[f, r]) * rates[r] for r in range(SPECIES)
        ]
        out[f, p, here] = flux[f] + half_gas * sum(parts[1:], parts[0])


def inner_kernel(
    rows, shares, old, flow_in, gap_in, rate, threshold, matrix, release,
    held, out, flow, gap, s_rate, s_threshold, s_matrix, s_release, sems,
):
    planes, height = old.shape[1:3]
    numbers = (s_rate, s_threshold, s_matrix, s_release)
    copies = fetch(
        (flow_in, gap_in, rate, threshold, matrix, release), (flow, gap) + numbers, sems
    )
    zeros = jnp.zeros((8, LANES), jnp.float32)

    def remap(j, carry):
        for f in range(FIELDS):
            held[f, j + 1, 0:8] = zeros
            held[f, j + 1, 8 + height : 16 + height] = zeros
            for b in range(height // 8):
                held[f, j + 1, pl.ds(8 + 8 * b, 8)] = mix(
                    [shares[j + 1, k] for k in range(SHIFT + 1)],
                    [old[f, j + k, pl.ds(8 * b, 8)] for k in range(SHIFT + 1)],
                )
        return carry

    lax.fori_loop(0, planes - SHIFT, remap, 0)
    for f in range(FIELDS):
        for b in range(height // 8):
            for j in (0, planes - SHIFT + 1):
                held[f, j, pl.ds(8 + 8 * b, 8)] = zeros
    for copy in copies:
        copy.wait()

    def step(p, carry):
        for b in range(height // 8):
            cells(rows, p, b, numbers, held, flow, gap, out)
        return carry

    lax.fori_loop(0, HEAD, step, 0)


def middle_kernel(
    rows, held, out_in, flow, gap, rate, threshold, matrix, release, out, s_rate, s_threshold,
    s_matrix, s_release, sems,
):
    planes, height = out.shape[1:3]
    numbers = (s_rate, s_threshold, s_matrix, s_release)
    for copy in fetch((rate, threshold, matrix, release), numbers, sems):
        copy.wait()

    def step(p, carry):
        for b in range(height // 8):
            cells(rows, p, b, numbers, held, flow, gap, out)
        return carry

    lax.fori_loop(HEAD, planes - SHIFT, step, 0)


def outer_kernel(
    rows, shares, old, upper, lower, held_in, out_in, flow, gap, rate, threshold, matrix,
    release, held, out, s_rate, s_threshold, s_matrix, s_release, sems,
):
    planes, height = old.shape[1:3]
    numbers = (s_rate, s_threshold, s_matrix, s_release)
    copies = fetch((rate, threshold, matrix, release), numbers, sems)
    zeros = jnp.zeros((8, LANES), jnp.float32)

    def remap(f, carry):
        for j in range(planes - SHIFT, planes):
            held[f, j + 1, 0:8] = zeros
            held[f, j + 1, 8 + height : 16 + height] = zeros
        for b in range(height // 8):
            here, body = pl.ds(8 * b, 8), pl.ds(8 + 8 * b, 8)

            def put(j, values):
                held[f, j + 1, body] = mix([shares[j + 1, k] for k in range(SHIFT + 1)], values)

            put(-1, [lower[f, here], old[f, 0, here], old[f, 1, here]])
            chain = [old[f, planes - SHIFT + p, here] for p in range(SHIFT)]
            chain += [upper[f, p, here] for p in range(SHIFT + 1)]
            for j in range(SHIFT + 1):
                put(planes - SHIFT + j, chain[j : j + 3])
        return carry

    lax.fori_loop(0, FIELDS, remap, 0)
    for copy in copies:
        copy.wait()

    for b in range(height // 8):
        here, body = pl.ds(8 * b, 8), pl.ds(8 + 8 * b, 8)
        for p, j, sign in ((0, 0, 0.1), (planes - SHIFT - 1, planes - SHIFT + 1, -0.1)):
            slope = 0.1 + sign * flow[0, p, here]
            for f in range(FIELDS):
                out[f, p, here] = out[f, p, here] + slope * held[f, j, body]

    def step(p, carry):
        for b in range(height // 8):
            cells(rows, p, b, numbers, held, flow, gap, out)
        return carry

    lax.fori_loop(planes - SHIFT, planes, step, 0)


def add_rows(rows, f, p, sides, flow, one, two, i, out):
    tiles = one.shape[1]
    even, low, high = sides
    for y, keep, sign, value in (
        (rows - 1, high, -1.0, jnp.where(even, one[i], two[i])),
        (0, low, 1.0, jnp.where(even, two[i], one[i])),
    ):
        where = pl.ds(y, tiles, stride=rows)
        slope = keep + (sign * keep) * flow[1, p, where, :]
        out[f, p, where, :] = out[f, p, where, :] + slope * value


def sides_of():
    place = lax.axis_index("xs")
    low = jnp.where(place > 0, 0.1, 0.0)
    high = jnp.where(place < lax.axis_size("xs") - 1, 0.1, 0.0)
    return lax.rem(place, 2) == 0, low, high


def glow_kernel(rows, scale, part_in, flow, gap, e1, o1, e2, o2, part, *rest):
    *outs, picture = rest
    planes, height = part.shape[1:3]
    sides = sides_of()
    first, middle, _, _ = rows_sent(planes)
    for listed, one, two in ((first[: 2 * (planes - SHIFT)], e1, o1), (middle, e2, o2)):
        for i, (f, p) in enumerate(listed):
            add_rows(rows, f, p, sides, flow, one, two, i, part)
    for b in range(height // 8):
        here = pl.ds(8 * b, 8)
        total = jnp.zeros((8, LANES), jnp.float32)
        for p in range(planes):
            gas = (1 - gap[p, here]).astype(jnp.float32)
            total += gas * part[GLOW, p, here] * part[SPECIES, p, here]
        picture[here, :] = total * scale
    split_rows(picture, outs, height, lax.axis_size("ax") // 2)


def error_kernel(kept, got, viewer, out, stage, sem):
    stage[...] = kept[...] + got[...] - viewer[...]
    copy = pltpu.make_async_copy(stage, out, sem)
    copy.start()
    copy.wait()


def store_kernel(rows, last, part_in, flow, one, two, *rest):
    part, final, thermal, sems = rest[-4:]
    planes, _ = part.shape[1:3]
    sides = sides_of()
    ready = planes - SHIFT
    now, _, late, late_ends = rows_sent(planes)
    listed = late + late_ends if last else now
    ends, most, everything = pl.ds(ready, SHIFT), pl.ds(0, ready), pl.ds(0, planes)
    if last:
        done = [(f, everything) for f in ORDER[EARLY:]] + [(f, ends) for f in ORDER[2:EARLY]]
    else:
        done = [(f, everything) for f in ORDER[:2]] + [(f, most) for f in ORDER[2:EARLY]]
    copies = []
    for n, (f, span) in enumerate(done):
        for i, (field, p) in enumerate(listed):
            if field == f and f not in ORDER[:2]:
                add_rows(rows, f, p, sides, flow, one, two, i, part)
        target = thermal if f == SPECIES else final.at[f]
        copies.append(pltpu.make_async_copy(part.at[f, span], target.at[span], sems.at[n]))
        copies[-1].start()
    for copy in copies:
        copy.wait()


def split_rows(picture, outs, height, stage):
    if len(outs) == 1:
        outs[0][...] = picture[...]
        return
    half = height // 2
    upper = lax.rem(lax.axis_index("ax") // stage, 2)
    for keep, out in zip((upper, 1 - upper), outs):
        out[...] = picture[pl.ds(pl.multiple_of(keep * half, 8), half), :]


def join_kernel(stage, kept, got, *rest):
    *outs, picture = rest
    picture[...] = kept[...] + got[...]
    split_rows(picture, outs, picture.shape[0], stage)


def call(kernel, args, outs, scratch=(), aliases=None, us=1):
    spaces = {"v": pltpu.VMEM, "h": pltpu.HBM}
    return pl.pallas_call(
        kernel,
        out_shape=tuple(spaces[m](shape, jnp.float32) if m != "g" else jax.ShapeDtypeStruct(shape, jnp.int32) for shape, m in outs),
        in_specs=[pl.BlockSpec(memory_space=spaces[m]) for _, m in args],
        out_specs=tuple(pl.BlockSpec(memory_space=spaces.get(m, pltpu.VMEM)) for _, m in outs),
        scratch_shapes=list(scratch),
        input_output_aliases=aliases or {},
        cost_estimate=pl.CostEstimate(flops=int(us * FLOPS), bytes_accessed=0, transcendentals=0),
        compiler_params=pltpu.CompilerParams(vmem_limit_bytes=GRANT),
    )(*(pltpu.with_memory_space_constraint(a, spaces[m]) for a, m in args))


def per_device(c, t, flow, gap, owner, rate, threshold, matrix, release, viewer):
    rows = t.shape[1]
    c_rows, t_rows = c, t
    c, t, flow, gap = (tiled(x) for x in (c, t, flow, gap))
    planes, height, _ = t.shape
    tiles = height // rows
    count = lax.axis_size("ax")
    first, middle, last, last_late = rows_sent(planes)
    first, middle, last = (
        ((len(x), tiles, LANES), "v") for x in (first, middle, last + last_late)
    )
    ends = ((FIELDS, SHIFT + 1, height, LANES), "v")
    whole = ((FIELDS, planes, height, LANES), "v")
    padded = ((FIELDS, planes + 2, height + 16, LANES), "v")
    numbers = [(x, "h") for x in (rate, threshold, matrix, release)]
    number_slots = [pltpu.SMEM(x.shape, x.dtype) for x, _ in numbers]
    sems = pltpu.SemaphoreType.DMA
    bind = functools.partial

    to_even, shares = call(
        bind(send_kernel, rows), [(c_rows, "h"), (t_rows, "h"), (owner, "h")],
        [first, ((planes + 2, SHIFT + 1, 8, LANES), "v")],
        [pltpu.SMEM(owner.shape, owner.dtype),
         pltpu.VMEM((EARLY, planes, 1, t_rows.shape[2]), jnp.float32), sems((FIELDS + 1,))],
    )
    to_odd, last_even, last_odd, lips, up, down, old = call(
        bind(more_kernel, rows), [(c, "h"), (t, "h"), (shares, "v")],
        [first, last, last, ((FIELDS * SHIFT * 2, tiles, LANES), "v"), ends,
         ((FIELDS, height, LANES), "v"), whole],
        [sems((FIELDS,))],
    )
    tiling = lax.axis_size("xs")
    xs_even, xs_odd = swaps(count, tiling, 0), swaps(count, tiling, 1)
    lips = lax.ppermute(lips, "ax", ring(count, -1))
    upper = lax.ppermute(up, "ax", ring(count, -1))
    e1 = lax.ppermute(to_even, ("ax", "xs"), xs_even)
    o1 = lax.ppermute(to_odd, ("ax", "xs"), xs_odd)
    lower = lax.ppermute(down, "ax", ring(count, 1))
    held, part, flow_v, gap_v = call(
        bind(inner_kernel, rows),
        [(shares, "v"), (old, "v"), (flow, "h"), (gap, "h")] + numbers,
        [padded, whole, (flow.shape, "v"), (gap.shape, "g")],
        number_slots + [sems((6,))], us=4,
    )
    late_even, late_odd, last_even, last_odd = call(
        bind(late_kernel, rows),
        [(shares, "v"), (old, "v"), (lips, "v"), (last_even, "v"), (last_odd, "v")],
        [middle, middle, last, last], (), {3: 2, 4: 3},
    )
    e2 = lax.ppermute(late_even, ("ax", "xs"), xs_even)
    o2 = lax.ppermute(late_odd, ("ax", "xs"), xs_odd)
    e3 = lax.ppermute(last_even, ("ax", "xs"), xs_even)
    o3 = lax.ppermute(last_odd, ("ax", "xs"), xs_odd)
    (part,) = call(
        bind(middle_kernel, rows),
        [(held, "v"), (part, "v"), (flow_v, "v"), (gap_v, "v")] + numbers,
        [whole], number_slots + [sems((4,))], {1: 0}, us=2,
    )
    held, part = call(
        bind(outer_kernel, rows),
        [(shares, "v"), (old, "v"), (upper, "v"), (lower, "v"), (held, "v"), (part, "v"),
         (flow_v, "v"), (gap_v, "v")] + numbers,
        [padded, whole], number_slots + [sems((4,))], {4: 0, 5: 1}, us=2,
    )
    final_shape = (SPECIES, planes, height, LANES)
    thermal_shape = (planes, height, LANES)
    direct = count & (count - 1) == 0 and tiles % count == 0
    pieces = 2 if direct else 1
    part, *glows = call(
        bind(glow_kernel, rows, 1.0 / owner.shape[0]),
        [(part, "v"), (flow_v, "v"), (gap_v, "v"), (e1, "v"), (o1, "v"), (e2, "v"), (o2, "v")],
        [whole] + [((height // pieces, LANES), "v")] * pieces,
        [pltpu.VMEM((height, LANES), jnp.float32)], {0: 0},
    )
    stores = [whole, (final_shape, "h"), (thermal_shape, "h")]
    part, final, thermal = call(
        bind(store_kernel, rows, False),
        [(part, "v"), (flow_v, "v"), (e1, "v"), (o1, "v")],
        stores, [sems((FIELDS,))], {0: 0},
    )
    part, final, thermal = call(
        bind(store_kernel, rows, True),
        [(part, "v"), (flow_v, "v"), (e3, "v"), (o3, "v"), (final, "h"), (thermal, "h")],
        stores, [sems((FIELDS,))], {0: 0, 4: 1, 5: 2},
    )
    place = lax.axis_index("ax")
    if direct:
        stage = count // 2
        while True:
            pairs = [(i, i ^ stage) for i in range(count)]
            kept, got = glows[0], lax.ppermute(glows[1], "ax", pairs)
            if stage == 1:
                break
            stage //= 2
            size = kept.shape[0]
            glows = call(
                bind(join_kernel, stage), [(kept, "v"), (got, "v")],
                [((size // 2, LANES), "v")] * 2, [pltpu.VMEM((size, LANES), jnp.float32)],
            )
        (error,) = call(
            error_kernel, [(kept, "v"), (got, "v"), (tiled(viewer), "v")],
            [(kept.shape, "h")], [pltpu.VMEM(kept.shape, jnp.float32), sems],
        )
        error = untiled(error, rows)
    else:
        picture = lax.psum(untiled(glows[0], rows), "ax")
        columns = picture.shape[1] // count
        mine = lax.dynamic_slice_in_dim(picture, place * columns, columns, 1)
        error = mine - viewer
    return untiled(final, rows), untiled(thermal, rows), error


def solution(mesh):
    volume, field = P(None, "ax", "xs", None), P("ax", "xs", None)
    in_specs = (volume, field, volume, field, P(), P(), P(), P(), P(), P("xs", "ax"))
    return jax.shard_map(
        per_device,
        mesh=mesh,
        in_specs=in_specs,
        out_specs=(volume, field, P("xs", "ax")),
        check_vma=False,
    )
```
